32 devices in a mesh: pipe: 2 (over core), ctx: 4 (over z), wa: 4 (over y, x).
Axes of the slice: x: 2, y: 2, z: 4, core: 2. Of those that a mesh axis runs over, the one named last changes fastest.
Arguments:
- section_inputs: bfloat16 [2, 2, 512, 1088], P('pipe', None, 'ctx'), may hold values from -6 to 6
- qkv_weight: bfloat16 [2, 17, 1088, 192], P('pipe', None, ('ctx', 'wa')), may hold values from -0.1875 to 0.1875
- out_weight: bfloat16 [2, 17, 1088, 64], P('pipe', None, ('ctx', 'wa')), may hold values from -6 to 6
- head_bias: float32 [2, 17, 128], P('pipe'), may hold values from -3 to 3
- mlp_weight: bfloat16 [2, 2, 1088, 4352], P('pipe', None, 'ctx', 'wa'), may hold values from -0.1875 to 0.1875
- hidden_bias: float32 [2, 4352], P('pipe', 'wa'), may hold values from -3 to 3
- feature_bias: float32 [2, 4, 1088], P('pipe'), may hold values from -3 to 3
- ln_gain: float32 [2, 2, 1088], P('pipe'), may hold values from 0.25 to 1.75
- block_table: int32 [4, 2], replicated, may hold values from 0 to 7, as said below
Outputs:
- section_outputs: float32 [2, 2, 512, 1088], P('pipe', None, 'ctx')
- qkv_grad: float32 [2, 17, 1088, 192], P('pipe', None, ('ctx', 'wa'))
- out_grad: float32 [2, 17, 1088, 64], P('pipe', None, ('ctx', 'wa'))
- head_bias_grad: float32 [2, 17, 128], P('pipe')
- mlp_grad: float32 [2, 2, 1088, 4352], P('pipe', None, 'ctx', 'wa')
- hidden_bias_grad: float32 [2, 4352], P('pipe', 'wa')
- feature_bias_grad: float32 [2, 4, 1088], P('pipe')
- ln_gain_grad: float32 [2, 2, 1088], P('pipe')
The draws below stay inside these ranges and needn't reach their ends.
Inputs may be any that keep to these rules, and one draw needn't show every extreme that they name: `block_table`: row c names a block b of 64 positions, b below 4, and its mirror 2 * 4 - 1 - b; every block appears once.
All inputs are finite; a program needn't handle non-finite values.
Results may differ from the reference program's by a relative error of at most 0.02.
Values may be sent and summed in bfloat16 or wider, within the bound.
A program may use at most 192 MiB of HBM per device.

```python
import math
import jax
import jax.numpy as jnp
from jax import lax

D = 1088
HEADS = 17
HD = 64
FF = 4352
MICRO = 2
BLOCK = 64
SEQ = 512
N_PIPE = 2
N_CTX = 4


def draw_block_table(key, part):
    order = jax.random.permutation(key, N_CTX).astype(jnp.int32)
    return jnp.stack([order, 2 * N_CTX - 1 - order], axis=1).astype(jnp.int32)


def steps_of(rng, shape, cuts, smallest, largest):
    level = 1.0
    for axis_at, shards_of in cuts:
        heights = jax.random.uniform(jax.random.fold_in(jax.random.fold_in(rng, 6), axis_at), (shards_of,), jnp.float32, smallest / len(cuts), largest / len(cuts))
        level = level * jnp.repeat(jnp.exp(heights), shape[axis_at] // shards_of).reshape((-1,) + (1,) * (len(shape) - 1 - axis_at))
    return level


def gaussian(key, dims, scale, reach, cuts=(), kind=jnp.bfloat16):
    level = steps_of(key, dims, cuts, -0.22, 0.18) if cuts else 1.0
    entries = jax.random.normal(key, dims, jnp.float32) * scale * level
    return jnp.minimum(jnp.maximum(entries, -reach), reach).astype(kind)


def setup_inputs(seed: int = 0) -> dict:
    key_list = jax.random.split(jax.random.key(seed), 10)
    section_inputs = gaussian(key_list[0], (N_PIPE, MICRO, SEQ, D), 1.0, 6.0, ((0, 2), (2, 4)))
    qkv_weight = gaussian(key_list[1], (N_PIPE, HEADS, D, 3 * HD), D ** -0.5, 0.1875, ((0, 2), (2, 16)))
    out_weight = gaussian(key_list[2], (N_PIPE, HEADS, D, HD), 1.0, 6.0, ((0, 2), (2, 16)))
    head_bias = gaussian(key_list[3], (N_PIPE, HEADS, 2 * HD), 0.5, 3.0, ((0, 2),), jnp.float32)
    mlp_weight = gaussian(key_list[4], (N_PIPE, 2, D, FF), D ** -0.5, 0.1875, ((0, 2), (2, 4), (3, 4)))
    hidden_bias = gaussian(key_list[5], (N_PIPE, FF), 0.5, 3.0, ((0, 2), (1, 4)), jnp.float32)
    feature_bias = gaussian(key_list[6], (N_PIPE, 4, D), 0.5, 3.0, ((0, 2),), jnp.float32)
    ln_gain = jnp.clip(1.0 + 0.15 * jax.random.normal(key_list[7], (N_PIPE, 2, D), jnp.float32), 0.25, 1.75)
    block_table = draw_block_table(jax.random.fold_in(key_list[9], 71), 0)
    return dict(section_inputs=section_inputs, qkv_weight=qkv_weight, out_weight=out_weight, head_bias=head_bias, mlp_weight=mlp_weight, hidden_bias=hidden_bias, feature_bias=feature_bias, ln_gain=ln_gain, block_table=block_table)


EPS = 1e-05
GELU_C = 0.7978845608028654
GELU_A = 0.044715

def norm_forward(stream, gain, offset):
    centre = lax.optimization_barrier(jnp.mean(stream, axis=-1, keepdims=True))
    centred = stream - centre
    variance = lax.optimization_barrier(jnp.mean(centred * centred, axis=-1, keepdims=True))
    inv_std = lax.rsqrt(variance + EPS)
    normed = centred * inv_std
    return (normed * gain + offset, normed, inv_std)

def norm_backward(grad_out, normed, inv_std, gain):
    grad_normed = grad_out * gain
    first_mean = lax.optimization_barrier(jnp.mean(grad_normed, axis=-1, keepdims=True))
    second_mean = lax.optimization_barrier(jnp.mean(grad_normed * normed, axis=-1, keepdims=True))
    return inv_std * (grad_normed - first_mean - normed * second_mean)

def gelu_value(hidden):
    tangent = jnp.tanh(GELU_C * (hidden + GELU_A * hidden * hidden * hidden))
    return 0.5 * hidden * (1.0 + tangent)

def gelu_slope(hidden):
    tangent = jnp.tanh(GELU_C * (hidden + GELU_A * hidden * hidden * hidden))
    return 0.5 * (1.0 + tangent) + 0.5 * hidden * (1.0 - tangent * tangent) * GELU_C * (1.0 + 3.0 * GELU_A * hidden * hidden)

def positions(block_table):
    starts = jnp.repeat(block_table.reshape(-1).astype(jnp.int32) * BLOCK, BLOCK)
    return starts + jnp.tile(jnp.arange(BLOCK, dtype=jnp.int32), 2 * N_CTX)

def block_layout():
    query_rows = math.gcd(SEQ, 512)
    return (query_rows, SEQ // query_rows)

def masked_scores(query_block, pos_block, key_wide, seq_pos):
    scores = jnp.einsum('hqe,hke->hqk', query_block.astype(jnp.float32), key_wide) * HD ** (-0.5)
    return jnp.where(seq_pos[None, None, :] <= pos_block[None, :, None], scores, -jnp.inf)

def layer_forward(layer_in, seq_pos, params):
    qkv_layer, out_layer, bias_heads, mlp_layer, bias_hidden, bias_feature, gain_layer = params
    query_rows, block_count = block_layout()
    stream = layer_in.astype(jnp.float32)
    normed_in, normed_one, inv_one = norm_forward(stream, gain_layer[0], bias_feature[0])
    attn_in = normed_in.astype(jnp.bfloat16)
    projected = jnp.einsum('td,hde->hte', attn_in.astype(jnp.float32), qkv_layer.astype(jnp.float32))
    queries = (projected[:, :, :HD] + bias_heads[:, None, :HD]).astype(jnp.bfloat16)
    key_rows = projected[:, :, HD:2 * HD].astype(jnp.bfloat16)
    values = (projected[:, :, 2 * HD:] + bias_heads[:, None, HD:]).astype(jnp.bfloat16)
    key_wide = key_rows.astype(jnp.float32)
    value_wide = values.astype(jnp.float32)
    query_blocks = queries.reshape(HEADS, block_count, query_rows, HD).transpose(1, 0, 2, 3)
    pos_blocks = seq_pos.reshape(block_count, query_rows)

    def attend(block_item):
        query_block, pos_block = block_item
        scores = masked_scores(query_block, pos_block, key_wide, seq_pos)
        row_top = lax.optimization_barrier(jnp.max(scores, axis=-1, keepdims=True))
        log_total = row_top + jnp.log(lax.optimization_barrier(jnp.sum(jnp.exp(scores - row_top), axis=-1, keepdims=True)))
        probs = jnp.exp(scores - log_total).astype(jnp.bfloat16)
        mixed_rows = jnp.einsum('hqk,hke->hqe', probs.astype(jnp.float32), value_wide).astype(jnp.bfloat16)
        return (mixed_rows, log_total[..., 0])
    mixed_blocks, total_blocks = lax.map(attend, (query_blocks, pos_blocks))
    mixed = mixed_blocks.transpose(1, 0, 2, 3).reshape(HEADS, SEQ, HD)
    log_total = total_blocks.transpose(1, 0, 2).reshape(HEADS, SEQ)
    attn_out = jnp.einsum('hte,hde->td', mixed.astype(jnp.float32), out_layer.astype(jnp.float32)) + bias_feature[1]
    first_sum = stream + attn_out
    normed_ffn, normed_two, inv_two = norm_forward(first_sum, gain_layer[1], bias_feature[2])
    ffn_in = normed_ffn.astype(jnp.bfloat16)
    pre = jnp.dot(ffn_in, mlp_layer[0], preferred_element_type=jnp.float32) + bias_hidden
    act = gelu_value(pre).astype(jnp.bfloat16)
    layer_out = first_sum + jnp.dot(act, mlp_layer[1].T, preferred_element_type=jnp.float32) + bias_feature[3]
    saved = (normed_one, inv_one, attn_in, queries, key_rows, values, mixed, log_total, normed_two, inv_two, ffn_in, pre, act)
    return (layer_out, saved)

def layer_backward(cot_low, seq_pos, saved, params):
    qkv_layer, out_layer, bias_heads, mlp_layer, bias_hidden, bias_feature, gain_layer = params
    normed_one, inv_one, attn_in, queries, key_rows, values, mixed, log_total, normed_two, inv_two, ffn_in, pre, act = saved
    query_rows, block_count = block_layout()
    cotangent = cot_low.astype(jnp.float32)
    grad_down = jnp.dot(cot_low.T, act, preferred_element_type=jnp.float32)
    d_act = jnp.dot(cot_low, mlp_layer[1], preferred_element_type=jnp.float32)
    d_pre = d_act * gelu_slope(pre)
    grad_hidden = lax.optimization_barrier(jnp.sum(d_pre, axis=0))
    d_pre_low = d_pre.astype(jnp.bfloat16)
    grad_up = jnp.dot(ffn_in.T, d_pre_low, preferred_element_type=jnp.float32)
    d_ffn = jnp.dot(d_pre_low, mlp_layer[0].T, preferred_element_type=jnp.float32)
    grad_gain_two = lax.optimization_barrier(jnp.sum(d_ffn * normed_two, axis=0))
    grad_shift_two = lax.optimization_barrier(jnp.sum(d_ffn, axis=0))
    d_first = cotangent + norm_backward(d_ffn, normed_two, inv_two, gain_layer[1])
    grad_attn_bias = lax.optimization_barrier(jnp.sum(d_first, axis=0))
    d_first_low = d_first.astype(jnp.bfloat16)
    grad_out = jnp.einsum('ti,hte->hie', d_first_low.astype(jnp.float32), mixed.astype(jnp.float32))
    d_mixed = jnp.einsum('ti,hie->hte', d_first_low.astype(jnp.float32), out_layer.astype(jnp.float32)).astype(jnp.bfloat16)
    key_wide = key_rows.astype(jnp.float32)
    value_wide = values.astype(jnp.float32)
    query_blocks = queries.reshape(HEADS, block_count, query_rows, HD).transpose(1, 0, 2, 3)
    dmix_blocks = d_mixed.reshape(HEADS, block_count, query_rows, HD).transpose(1, 0, 2, 3)
    total_blocks = log_total.reshape(HEADS, block_count, query_rows).transpose(1, 0, 2)
    pos_blocks = seq_pos.reshape(block_count, query_rows)

    def step_back(carry, block_item):
        key_acc, value_acc = carry
        query_block, dmix_block, total_block, pos_block = block_item
        scores = masked_scores(query_block, pos_block, key_wide, seq_pos)
        probs = jnp.exp(scores - total_block[..., None])
        d_probs = jnp.einsum('hqe,hke->hqk', dmix_block.astype(jnp.float32), value_wide)
        delta = lax.optimization_barrier(jnp.sum(probs * d_probs, axis=-1, keepdims=True))
        d_scores = (probs * (d_probs - delta) * HD ** (-0.5)).astype(jnp.bfloat16)
        d_query_block = jnp.einsum('hqk,hke->hqe', d_scores.astype(jnp.float32), key_wide)
        key_acc = key_acc + jnp.einsum('hqk,hqe->hke', d_scores.astype(jnp.float32), query_block.astype(jnp.float32))
        value_acc = value_acc + jnp.einsum('hqk,hqe->hke', probs.astype(jnp.bfloat16).astype(jnp.float32), dmix_block.astype(jnp.float32))
        return ((key_acc, value_acc), d_query_block)
    start = (jnp.zeros((HEADS, SEQ, HD), jnp.float32), jnp.zeros((HEADS, SEQ, HD), jnp.float32))
    (d_key, d_value), dq_blocks = lax.scan(step_back, start, (query_blocks, dmix_blocks, total_blocks, pos_blocks))
    d_query = dq_blocks.transpose(1, 0, 2, 3).reshape(HEADS, SEQ, HD)
    grad_heads = jnp.concatenate([lax.optimization_barrier(jnp.sum(d_query, axis=1)), lax.optimization_barrier(jnp.sum(d_value, axis=1))], axis=-1)
    d_proj = jnp.concatenate([d_query.astype(jnp.bfloat16), d_key.astype(jnp.bfloat16), d_value.astype(jnp.bfloat16)], axis=-1)
    grad_qkv = jnp.einsum('td,hte->hde', attn_in.astype(jnp.float32), d_proj.astype(jnp.float32))
    d_attn = jnp.einsum('hte,hde->td', d_proj.astype(jnp.float32), qkv_layer.astype(jnp.float32))
    grad_gain_one = lax.optimization_barrier(jnp.sum(d_attn * normed_one, axis=0))
    grad_shift_one = lax.optimization_barrier(jnp.sum(d_attn, axis=0))
    d_input = d_first + norm_backward(d_attn, normed_one, inv_one, gain_layer[0])
    grad_feature = jnp.stack([grad_shift_one, grad_attn_bias, grad_shift_two, lax.optimization_barrier(jnp.sum(cotangent, axis=0))])
    grad_gains = jnp.stack([grad_gain_one, grad_gain_two])
    grads = (grad_qkv, grad_out, grad_heads, jnp.stack([grad_up, grad_down]), grad_hidden, grad_feature, grad_gains)
    return (d_input, grads)

def reference(section_inputs, qkv_weight, out_weight, head_bias, mlp_weight, hidden_bias, feature_bias, ln_gain, block_table):
    seq_pos = positions(block_table)
    layer_params = []
    for layer in range(2):
        layer_params.append((qkv_weight[layer], out_weight[layer], head_bias[layer], mlp_weight[layer], hidden_bias[layer], feature_bias[layer], ln_gain[layer]))
    totals = [None, None]
    outputs_last = []
    input_grads = []
    for batch in range(MICRO):
        first_out, first_saved = layer_forward(section_inputs[0, batch], seq_pos, layer_params[0])
        middle = lax.optimization_barrier(first_out.astype(jnp.bfloat16))
        last_out, last_saved = layer_forward(middle, seq_pos, layer_params[1])
        outputs_last.append(last_out)
        back_grad, last_grads = layer_backward(section_inputs[1, batch], seq_pos, last_saved, layer_params[1])
        back_low = lax.optimization_barrier(back_grad.astype(jnp.bfloat16))
        input_grad, first_grads = layer_backward(back_low, seq_pos, first_saved, layer_params[0])
        input_grads.append(input_grad)
        for layer, grads in ((0, first_grads), (1, last_grads)):
            if totals[layer] is None:
                totals[layer] = grads
            else:
                totals[layer] = jax.tree.map(jnp.add, totals[layer], grads)
    section_outputs = jnp.stack([jnp.stack(input_grads), jnp.stack(outputs_last)])
    joined = [jnp.stack([totals[0][index], totals[1][index]]) for index in range(7)]
    return (section_outputs, joined[0], joined[1], joined[2], joined[3], joined[4], joined[5], joined[6])
```

```python
import functools

import jax
import jax.numpy as jnp
from jax import lax
from jax.experimental import pallas as pl
from jax.experimental.pallas import tpu as pltpu
from jax.sharding import PartitionSpec as P

EPS = 1e-05
GELU_C = 0.7978845608028654
GELU_A = 0.044715
KERNELS = True
MESH = pl.DeviceIdType.MESH
VM = pl.BlockSpec(memory_space=pltpu.VMEM)
IDS = {"sum_wa": 1, "swap_wa": 2, "swap_ctx": 3, "line_attn": 4, "line_mlp": 5, "line_pair": 6, "swap_mlp": 7,
       "swap_attn": 8, "all_small": 9, "all_heads": 10, "swap_grad": 11}


def remote(src, dst, send, recv, peer):
    return pltpu.make_async_remote_copy(
        src_ref=src, dst_ref=dst, send_sem=send, recv_sem=recv, device_id=peer, device_id_type=MESH
    )


def greet(peers):
    barrier = pltpu.get_barrier_semaphore()
    for peer in peers:
        pl.semaphore_signal(barrier, inc=1, device_id=peer, device_id_type=MESH)
    pl.semaphore_wait(barrier, len(peers))


def sum_kernel(axis, n, x_ref, o_ref, got, send_a, recv_a, send_b, recv_b):
    me = lax.axis_index(axis)
    peers = [{axis: lax.rem(me + d, n)} for d in range(1, n)]
    greet(peers)
    first = [
        remote(x_ref.at[lax.rem(me + d, n)], got.at[d - 1], send_a.at[d - 1], recv_a.at[d - 1], peers[d - 1])
        for d in range(1, n)
    ]
    for copy in first:
        copy.start()
    total = x_ref[me].astype(jnp.float32)
    for d, copy in enumerate(first):
        copy.wait_recv()
        total = total + got[d].astype(jnp.float32)
    o_ref[me] = total.astype(o_ref.dtype)
    second = [
        remote(o_ref.at[me], o_ref.at[me], send_b.at[d - 1], recv_b.at[d - 1], peers[d - 1]) for d in range(1, n)
    ]
    for copy in second:
        copy.start()
    for copy in first:
        copy.wait_send()
    for copy in second:
        copy.wait()


def swap_kernel(axis, n, x_ref, o_ref, send, recv, local):
    me = lax.axis_index(axis)
    peers = [{axis: lax.rem(me + d, n)} for d in range(1, n)]
    greet(peers)
    copies = [
        remote(x_ref.at[lax.rem(me + d, n)], o_ref.at[me], send.at[d - 1], recv.at[d - 1], peers[d - 1])
        for d in range(1, n)
    ]
    for copy in copies:
        copy.start()
    own = pltpu.make_async_copy(x_ref.at[me], o_ref.at[me], local)
    own.start()
    own.wait()
    for copy in copies:
        copy.wait()


def all_kernel(axis, n, x_ref, o_ref, send, recv, local):
    me = lax.axis_index(axis)
    peers = [{axis: lax.rem(me + d, n)} for d in range(1, n)]
    greet(peers)
    copies = [
        remote(x_ref, o_ref.at[me], send.at[d - 1], recv.at[d - 1], peers[d - 1]) for d in range(1, n)
    ]
    for copy in copies:
        copy.start()
    own = pltpu.make_async_copy(x_ref, o_ref.at[me], local)
    own.start()
    own.wait()
    for copy in copies:
        copy.wait()


def line_kernel(n, both, x_ref, o_ref, send_r, recv_r, send_l, recv_l, send_p, recv_p, local):
    me = lax.axis_index("ctx")
    side = lax.axis_index("pipe")
    row = side if both else 0
    right, left, mate = {"ctx": me + 1}, {"ctx": me - 1}, {"pipe": 1 - side}
    barrier = pltpu.get_barrier_semaphore()
    not_last, not_first = me + 1 < n, me > 0

    @pl.when(not_last)
    def _():
        pl.semaphore_signal(barrier, inc=1, device_id=right, device_id_type=MESH)

    @pl.when(not_first)
    def _():
        pl.semaphore_signal(barrier, inc=1, device_id=left, device_id_type=MESH)

    if both:
        pl.semaphore_signal(barrier, inc=1, device_id=mate, device_id_type=MESH)
    extra = 1 if both else 0

    @pl.when(not_first & not_last)
    def _():
        pl.semaphore_wait(barrier, 2 + extra)

    @pl.when(jnp.logical_not(not_first & not_last))
    def _():
        pl.semaphore_wait(barrier, 1 + extra)

    own = pltpu.make_async_copy(x_ref, o_ref.at[row, me], local)
    own.start()

    def block(at, fresh):
        return x_ref if fresh else o_ref.at[row, at]

    def to_right(s):
        return remote(block(me - s, s == 0), o_ref.at[row, me - s], send_r.at[s], recv_r.at[s], right)

    def to_left(s):
        return remote(block(me + s, s == 0), o_ref.at[row, me + s], send_l.at[s], recv_l.at[s], left)

    def to_mate(at, fresh):
        return remote(block(at, fresh), o_ref.at[row, at], send_p.at[at], recv_p.at[at], mate)

    def arrived(at, sem):
        return remote(o_ref.at[row, at], o_ref.at[row, at], send_r.at[0], sem, mate)

    for s in range(n):

        @pl.when(me - s >= 0)
        def _():
            if s > 0:
                arrived(me - s, recv_r.at[s - 1]).wait_recv()
            if s < n - 1:

                @pl.when(not_last)
                def _():
                    to_right(s).start()

            if both and s > 0:
                to_mate(me - s, False).start()

        @pl.when(me + s < n)
        def _():
            if s > 0:
                arrived(me + s, recv_l.at[s - 1]).wait_recv()
            if s < n - 1:

                @pl.when(not_first)
                def _():
                    to_left(s).start()

            if both:
                to_mate(me + s, s == 0).start()

    own.wait()
    for s in range(n - 1):

        @pl.when((me - s >= 0) & not_last)
        def _():
            to_right(s).wait_send()

        @pl.when((me + s < n) & not_first)
        def _():
            to_left(s).wait_send()

    if both:
        for at in range(n):
            to_mate(at, False).wait_send()
            remote(o_ref.at[1 - side, at], o_ref.at[1 - side, at], send_p.at[at], recv_p.at[at], mate).wait_recv()


def call(kernel, name, shape, scratch, x):
    return pl.pallas_call(
        kernel,
        out_shape=jax.ShapeDtypeStruct(shape, x.dtype),
        in_specs=[VM],
        out_specs=VM,
        scratch_shapes=scratch,
        compiler_params=pltpu.CompilerParams(
            collective_id=IDS[name], has_side_effects=True, vmem_limit_bytes=60 * 1024 * 1024
        ),
        name=name,
    )(x)


def dma(count):
    return pltpu.SemaphoreType.DMA((count,))


def summed(x):
    n = lax.axis_size("wa")
    low = x.astype(jnp.bfloat16)
    if not KERNELS:
        return lax.psum(low.astype(jnp.float32), "wa").astype(jnp.bfloat16).astype(jnp.float32)
    parts = low.reshape(n, low.shape[0] // n, low.shape[1])
    scratch = [pltpu.VMEM((n - 1,) + parts.shape[1:], jnp.bfloat16)] + [dma(n - 1)] * 4
    out = call(functools.partial(sum_kernel, "wa", n), "sum_wa", parts.shape, scratch, parts)
    return out.reshape(low.shape).astype(jnp.float32)


def swapped(x, axis, name):
    n = lax.axis_size(axis)
    if not KERNELS:
        return lax.all_to_all(x, axis, split_axis=0, concat_axis=0, tiled=True)
    scratch = [dma(n - 1)] * 2 + [pltpu.SemaphoreType.DMA]
    return call(functools.partial(swap_kernel, axis, n), name, x.shape, scratch, x)


def gathered(x, axis, name):
    n = lax.axis_size(axis)
    if not KERNELS:
        return lax.all_gather(x, axis)
    scratch = [dma(n - 1)] * 2 + [pltpu.SemaphoreType.DMA]
    return call(functools.partial(all_kernel, axis, n), name, (n,) + x.shape, scratch, x)


def lined(x, both, name):
    n = lax.axis_size("ctx")
    if not KERNELS:
        out = lax.all_gather(x, "ctx")
        return lax.all_gather(out, "pipe") if both else out[None]
    scratch = [dma(n - 1)] * 4 + [dma(n)] * 2 + [pltpu.SemaphoreType.DMA]
    return call(functools.partial(line_kernel, n, both), name, (2 if both else 1, n) + x.shape, scratch, x)


def dot(a, b, ca, cb):
    return lax.dot_general(a, b, (((ca,), (cb,)), ((), ())), preferred_element_type=jnp.float32)


def attend_kernel(scale, qpos, kpos, q_ref, kv_ref, mix_ref, total_ref):
    heads = q_ref.shape[0]
    allowed = kpos[...] <= qpos[...]
    for h in range(heads):
        kv = kv_ref[:, h].reshape(-1, kv_ref.shape[-1])
        scores = jnp.where(allowed, dot(q_ref[h], kv, 1, 1) * scale, -jnp.inf)
        top = jnp.max(scores, axis=-1, keepdims=True)
        total = top + jnp.log(jnp.sum(jnp.exp(scores - top), axis=-1, keepdims=True))
        probs = jnp.exp(scores - total).astype(jnp.bfloat16)
        mix_ref[h] = dot(probs, kv, 1, 0).astype(jnp.bfloat16)
        total_ref[h] = total


def attend_back_kernel(scale, qpos, kpos, q_ref, kv_ref, dm_ref, total_ref, dq_ref, dkv_ref):
    heads = q_ref.shape[0]
    allowed = kpos[...] <= qpos[...]
    for h in range(heads):
        kv = kv_ref[:, h].reshape(-1, kv_ref.shape[-1])
        scores = jnp.where(allowed, dot(q_ref[h], kv, 1, 1) * scale, -jnp.inf)
        probs = jnp.exp(scores - total_ref[h])
        d_probs = dot(dm_ref[h], kv, 1, 1)
        delta = jnp.sum(probs * d_probs, axis=-1, keepdims=True)
        d_scores = (probs * (d_probs - delta) * scale).astype(jnp.bfloat16)
        dq_ref[h] = dot(d_scores, kv, 1, 0)
        d_kv = dot(d_scores, q_ref[h], 0, 0) + dot(probs.astype(jnp.bfloat16), dm_ref[h], 0, 0)
        dkv_ref[:, h] = d_kv.astype(jnp.bfloat16).reshape(dkv_ref.shape[0], dkv_ref.shape[2], dkv_ref.shape[3])


def local_call(kernel, shapes, *args):
    return pl.pallas_call(
        kernel,
        out_shape=[jax.ShapeDtypeStruct(*s) for s in shapes],
        in_specs=[VM] * len(args),
        out_specs=[VM] * len(shapes),
        compiler_params=pltpu.CompilerParams(vmem_limit_bytes=48 * 1024 * 1024),
        interpret=not KERNELS,
    )(*args)

def norm_forward(stream, gain, offset):
    centre = jnp.mean(stream, axis=-1, keepdims=True)
    centred = stream - centre
    variance = jnp.mean(centred * centred, axis=-1, keepdims=True)
    inv_std = lax.rsqrt(variance + EPS)
    normed = centred * inv_std
    return (normed * gain + offset, normed, inv_std)


def norm_backward(grad_out, normed, inv_std, gain):
    grad_normed = grad_out * gain
    first_mean = jnp.mean(grad_normed, axis=-1, keepdims=True)
    second_mean = jnp.mean(grad_normed * normed, axis=-1, keepdims=True)
    return inv_std * (grad_normed - first_mean - normed * second_mean)


def gelu_value(hidden):
    tangent = jnp.tanh(GELU_C * (hidden + GELU_A * hidden * hidden * hidden))
    return 0.5 * hidden * (1.0 + tangent)


def gelu_slope(hidden):
    tangent = jnp.tanh(GELU_C * (hidden + GELU_A * hidden * hidden * hidden))
    return 0.5 * (1.0 + tangent) + 0.5 * hidden * (1.0 - tangent * tangent) * GELU_C * (
        1.0 + 3.0 * GELU_A * hidden * hidden
    )


def per_device(
    section_inputs,
    qkv_weight,
    out_weight,
    head_bias,
    mlp_weight,
    hidden_bias,
    feature_bias,
    ln_gain,
    block_table,
):
    ctx_count = lax.axis_size("ctx")
    shard_count = lax.axis_size("wa")
    side = lax.axis_index("pipe")
    ctx_index = lax.axis_index("ctx")
    shard_index = lax.axis_index("wa")
    rows = section_inputs.shape[2]
    width = section_inputs.shape[3]
    head_count = qkv_weight.shape[1]
    head_dim = out_weight.shape[3]
    part = qkv_weight.shape[2]
    slots = (head_count + shard_count - 1) // shard_count
    pad = slots * shard_count - head_count
    block_rows = rows // 2
    scale = head_dim ** (-0.5)
    swap = [(0, 1), (1, 0)]
    low = jnp.bfloat16

    own_blocks = lax.dynamic_index_in_dim(block_table, ctx_index, 0, keepdims=False)
    step = jnp.arange(block_rows, dtype=jnp.int32)
    query_pos = (own_blocks[:, None] * block_rows + step[None, :]).reshape(rows, 1)
    key_pos = (block_table.reshape(-1)[:, None] * block_rows + step[None, :]).reshape(1, rows * ctx_count)

    def mine(first, second):
        return jnp.where(side == 0, first, second)

    inputs = section_inputs[0]
    traded = lax.ppermute(mine(inputs[1], inputs[0]), "pipe", swap)
    layer_input = mine(inputs[0], traded)
    last_cot = mine(traded, inputs[1])

    packed = jnp.concatenate([qkv_weight[0], out_weight[0]], axis=-1)
    packed = jnp.pad(packed, ((0, pad), (0, 0), (0, 0)))
    packed = packed.reshape(slots, shard_count, part, 4 * head_dim).transpose(1, 0, 2, 3)
    attn_all = lined(swapped(packed, "wa", "swap_wa"), True, "line_attn")
    mlp_all = lined(mlp_weight[0], True, "line_mlp")

    sizes = [head_bias[0].size, hidden_bias[0].size, feature_bias[0].size]
    small = jnp.concatenate(
        [head_bias[0].reshape(-1), hidden_bias[0], feature_bias[0].reshape(-1), ln_gain[0].reshape(-1)]
    )
    small_mate = lax.ppermute(small, "pipe", swap)

    def params_of(layer):
        weight = attn_all[layer].transpose(2, 0, 1, 3, 4).reshape(slots, width, 4 * head_dim)
        up = mlp_all[layer][:, 0].reshape(width, -1)
        down = mlp_all[layer][:, 1].reshape(width, -1)
        flat = jnp.where(side == layer, small, small_mate)
        heads, hidden, feature, gains = jnp.split(flat, [sizes[0], sizes[0] + sizes[1], sum(sizes)])
        heads = jnp.pad(heads.reshape(head_count, 2 * head_dim), ((0, pad), (0, 0)))
        heads = heads.reshape(slots, shard_count, 2 * head_dim)
        heads = lax.dynamic_index_in_dim(heads, shard_index, 1, keepdims=False)
        return (
            weight[:, :, : 3 * head_dim],
            weight[:, :, 3 * head_dim :],
            heads,
            up,
            down,
            hidden,
            feature.reshape(4, width),
            gains.reshape(2, width),
        )

    def widened(x, before):
        zero = jnp.zeros_like(x)
        return jnp.concatenate([zero, x] if before else [x, zero], axis=-1)

    def forward(layer_in, params):
        w_qkv, w_out, bias, w_up, w_down, bias_hidden, shifts, gains = params
        stream = layer_in.astype(jnp.float32)
        normed_in, normed_one, inv_one = norm_forward(stream, gains[0], shifts[0])
        attn_in = normed_in.astype(low)
        projected = jnp.einsum("td,hde->hte", attn_in, w_qkv, preferred_element_type=jnp.float32)
        queries = widened((projected[:, :, :head_dim] + bias[:, None, :head_dim]).astype(low), False)
        key_rows = projected[:, :, head_dim : 2 * head_dim].astype(low)
        values = (projected[:, :, 2 * head_dim :] + bias[:, None, head_dim:]).astype(low)
        pairs = lined(jnp.concatenate([key_rows, values], axis=-1), False, "line_pair")[0]
        mixed, log_total = local_call(
            functools.partial(attend_kernel, scale),
            [((slots, rows, 2 * head_dim), low), ((slots, rows, 1), jnp.float32)],
            query_pos,
            key_pos,
            queries,
            pairs,
        )
        mixed = mixed[:, :, head_dim:]
        attn_out = summed(jnp.einsum("hte,hde->td", mixed, w_out, preferred_element_type=jnp.float32))
        first_sum = stream + attn_out + shifts[1]
        normed_ffn, normed_two, inv_two = norm_forward(first_sum, gains[1], shifts[2])
        ffn_in = normed_ffn.astype(low)
        pre = jnp.dot(ffn_in, w_up, preferred_element_type=jnp.float32) + bias_hidden
        act = gelu_value(pre).astype(low)
        layer_out = (
            first_sum
            + summed(jnp.einsum("tf,df->td", act, w_down, preferred_element_type=jnp.float32))
            + shifts[3]
        )
        return layer_out, (
            normed_one, inv_one, attn_in, queries, pairs, mixed, log_total, normed_two, inv_two, ffn_in, pre, act,
        )

    def backward(cot, saved, params):
        w_qkv, w_out, bias, w_up, w_down, bias_hidden, shifts, gains = params
        normed_one, inv_one, attn_in, queries, pairs, mixed, log_total, normed_two, inv_two, ffn_in, pre, act = saved
        cotangent = cot.astype(jnp.float32)
        grad_down = jnp.einsum("ti,tf->if", cot, act, preferred_element_type=jnp.float32)
        d_act = jnp.einsum("ti,if->tf", cot, w_down, preferred_element_type=jnp.float32)
        d_pre = d_act * gelu_slope(pre)
        grad_hidden = jnp.sum(d_pre, axis=0)
        d_pre_low = d_pre.astype(low)
        grad_up = jnp.einsum("td,tf->df", ffn_in, d_pre_low, preferred_element_type=jnp.float32)
        d_ffn = summed(jnp.einsum("tf,df->td", d_pre_low, w_up, preferred_element_type=jnp.float32))
        d_first = cotangent + norm_backward(d_ffn, normed_two, inv_two, gains[1])
        d_first_low = d_first.astype(low)
        grad_out = jnp.einsum("ti,hte->hie", d_first_low, mixed, preferred_element_type=jnp.float32)
        d_mixed = jnp.einsum("ti,hie->hte", d_first_low, w_out, preferred_element_type=jnp.float32)
        d_query, pair_terms = local_call(
            functools.partial(attend_back_kernel, scale),
            [((slots, rows, 2 * head_dim), jnp.float32), (pairs.shape, low)],
            query_pos,
            key_pos,
            queries,
            pairs,
            widened(d_mixed.astype(low), True),
            log_total,
        )
        d_query = d_query[:, :, :head_dim]
        d_pair = swapped(pair_terms, "ctx", "swap_ctx").astype(jnp.float32).sum(axis=0)
        grad_heads = jnp.concatenate(
            [jnp.sum(d_query, axis=1), jnp.sum(d_pair[:, :, head_dim:], axis=1)], axis=-1
        )
        d_proj = jnp.concatenate([d_query.astype(low), d_pair.astype(low)], axis=-1)
        grad_qkv = jnp.einsum("td,hte->hde", attn_in, d_proj, preferred_element_type=jnp.float32)
        d_attn = summed(jnp.einsum("hte,hde->td", d_proj, w_qkv, preferred_element_type=jnp.float32))
        d_input = d_first + norm_backward(d_attn, normed_one, inv_one, gains[0])
        vectors = [
            jnp.sum(d_attn, axis=0),
            jnp.sum(d_first, axis=0),
            jnp.sum(d_ffn, axis=0),
            jnp.sum(cotangent, axis=0),
            jnp.sum(d_attn * normed_one, axis=0),
            jnp.sum(d_ffn * normed_two, axis=0),
            grad_hidden,
            grad_heads.reshape(-1),
        ]
        attn_grad = jnp.concatenate([grad_qkv, grad_out], axis=-1).astype(low)
        mlp_grad = jnp.stack([grad_up, grad_down]).astype(low)
        return d_input, attn_grad, mlp_grad, jnp.concatenate(vectors)

    params = [params_of(0), params_of(1)]
    first_out, first_saved = forward(layer_input, params[0])
    last_out, last_saved = forward(first_out.astype(low), params[1])
    back, attn_one, mlp_one, vec_one = backward(last_cot, last_saved, params[1])
    d_input, attn_zero, mlp_zero, vec_zero = backward(back.astype(low), first_saved, params[0])

    def over_pipe(zero, one):
        kept = mine(zero, one)
        got = lax.ppermute(mine(one, zero), "pipe", swap)
        return kept.astype(jnp.float32) + got.astype(jnp.float32)

    mlp_sum = over_pipe(mlp_zero, mlp_one).astype(low)
    mlp_sum = mlp_sum.reshape(2, ctx_count, width // ctx_count, -1).transpose(1, 0, 2, 3)
    mlp_out = swapped(mlp_sum, "ctx", "swap_mlp").astype(jnp.float32).sum(axis=0)

    attn_sum = over_pipe(attn_zero, attn_one).astype(low)
    attn_sum = attn_sum.reshape(slots, ctx_count, shard_count, part, 4 * head_dim).transpose(1, 2, 0, 3, 4)
    attn_part = swapped(attn_sum, "ctx", "swap_attn").astype(jnp.float32).sum(axis=0).astype(low)
    attn_out = swapped(attn_part, "wa", "swap_grad")
    attn_out = attn_out.transpose(1, 0, 2, 3).reshape(slots * shard_count, part, 4 * head_dim)
    attn_out = attn_out[:head_count].astype(jnp.float32)

    vec = over_pipe(vec_zero, vec_one)
    length = vec.shape[0]
    fill = -length % 128
    vec = jnp.pad(vec, (0, fill)).reshape(-1, 128)
    vec = gathered(vec, "ctx", "all_small").sum(axis=0).reshape(-1)[:length]
    feature_sum, gain_sum, hidden_own, head_own = jnp.split(
        vec, [4 * width, 6 * width, 6 * width + hidden_bias.shape[1]]
    )
    head_sum = gathered(head_own.reshape(slots, 2 * head_dim), "wa", "all_heads")
    head_sum = head_sum.transpose(1, 0, 2).reshape(slots * shard_count, 2 * head_dim)[:head_count]

    last_traded = lax.ppermute(mine(last_out, d_input), "pipe", swap)
    section_outputs = jnp.where(
        side == 0, jnp.stack([d_input, last_traded]), jnp.stack([last_traded, last_out])
    )
    return (
        section_outputs[None],
        attn_out[None, :, :, : 3 * head_dim],
        attn_out[None, :, :, 3 * head_dim :],
        head_sum[None],
        mlp_out[None],
        hidden_own[None],
        feature_sum.reshape(1, 4, width),
        gain_sum.reshape(1, 2, width),
    )


def solution(mesh):
    return jax.shard_map(
        per_device,
        mesh=mesh,
        in_specs=(
            P("pipe", None, "ctx", None),
            P("pipe", None, ("ctx", "wa"), None),
            P("pipe", None, ("ctx", "wa"), None),
            P("pipe", None, None),
            P("pipe", None, "ctx", "wa"),
            P("pipe", "wa"),
            P("pipe", None, None),
            P("pipe", None, None),
            P(),
        ),
        out_specs=(
            P("pipe", None, "ctx", None),
            P("pipe", None, ("ctx", "wa"), None),
            P("pipe", None, ("ctx", "wa"), None),
            P("pipe", None, None),
            P("pipe", None, "ctx", "wa"),
            P("pipe", "wa"),
            P("pipe", None, None),
            P("pipe", None, None),
        ),
        check_vma=False,
    )
```
